32 devices in a mesh: row: 4 (over x, core), col: 8 (over z, y).
Axes of the slice: x: 2, y: 2, z: 4, core: 2. Of those that a mesh axis runs over, the one named last changes fastest.
Arguments:
- fiber_rows: bfloat16 [16384, 1024], P(('row', 'col')), may hold values from -6 to 6
- fiber_i: int32 [16384], P(('row', 'col')), may hold values from 0 to 4095
- fiber_j: int32 [16384], P(('row', 'col')), may hold values from 0 to 65535, as said below
- fiber_count: int32 [32], P(('row', 'col')), may hold values from 256 to 512, as said below
- factor_two: bfloat16 [65536, 32], P('col'), may hold values from -1 to 1
Outputs:
- mode_one: bfloat16 [4096, 32768], P(('row', 'col'))
The draws below stay inside these ranges and needn't reach their ends.
Inputs may be any that keep to these rules, and one draw needn't show every extreme that they name: fiber_j of a slot on the device with index c along col lies in c * 8192 to (c + 1) * 8192 - 1. `fiber_count`: among the live slots of one device at most 32 have fiber_i in the block of 128 indices of one device (block fiber_i // 128, in the order row then col); some device is full and reaches 32 for each block it sends to.
All inputs are finite; a program needn't handle non-finite values.
Results may differ from the reference program's by a relative error of at most 0.001.
Values may be sent and summed in bfloat16 or wider, within the bound.
A program may use at most 128 MiB of HBM per device.

```python
import jax
import jax.numpy as jnp
from jax import lax

R = 32
RR = 1024
FIB_DEV = 512
I_DEV = 128
J_COL = 8192
FIBERS = 16384
I1 = 4096
I2 = 65536
N_ROW = 4
N_COL = 8


def fiber_layout(key):
    devices = N_ROW * N_COL
    base = jax.random.fold_in(key, 7)
    key_perm, key_sigma, key_count, key_full = jax.random.split(base, 4)
    perms = jax.vmap(lambda k: jax.random.permutation(k, FIB_DEV))(jax.random.split(key_perm, devices))
    sigmas = jax.vmap(lambda k: jax.random.permutation(k, devices))(jax.random.split(key_sigma, devices))
    bucket = (perms % (devices // 2)).astype(jnp.int32)
    targets = jnp.take_along_axis(sigmas, bucket, axis=1).astype(jnp.int32)
    counts = jax.random.randint(key_count, (devices,), FIB_DEV // 2, FIB_DEV + 1).astype(jnp.int32)
    full = jax.random.randint(key_full, (), 0, devices)
    counts = jnp.where(jnp.arange(devices) == full, FIB_DEV, counts).astype(jnp.int32)
    return (targets, counts)


def draw_fiber_i(key, part):
    devices = N_ROW * N_COL
    targets, counts = fiber_layout(key)
    offsets = jax.random.randint(jax.random.fold_in(key, 11), (devices, FIB_DEV), 0, I_DEV)
    return (targets * I_DEV + offsets).astype(jnp.int32).reshape(FIBERS)


def draw_fiber_j(key, part):
    devices = N_ROW * N_COL
    column = (jnp.arange(devices, dtype=jnp.int32) % N_COL)[:, None]
    offsets = jax.random.randint(jax.random.fold_in(key, 13), (devices, FIB_DEV), 0, J_COL)
    return (column * J_COL + offsets).astype(jnp.int32).reshape(FIBERS)


def draw_fiber_count(key, part):
    targets, counts = fiber_layout(key)
    return counts


def block_levels(rng, extent, shards, smallest, largest):
    def one(dim, shards_of):
        heights = jax.random.uniform(jax.random.fold_in(jax.random.fold_in(rng, 6), dim), (shards_of,), jnp.float32, smallest / len(shards), largest / len(shards))
        return jnp.repeat(jnp.exp(heights), extent[dim] // shards_of).reshape((-1,) + (1,) * (len(extent) - dim - 1))

    level = one(*shards[0])
    for cut in shards[1:]:
        level = level * one(*cut)
    return level


def bell_draw(rng, shape, deviation, reach, cuts=(), held_as=jnp.bfloat16):
    factor_of = block_levels(rng, shape, cuts, -0.22, 0.18) if cuts else 1.0
    values = jax.random.normal(rng, shape, jnp.float32) * deviation * factor_of
    return jnp.minimum(jnp.maximum(values, -reach), reach).astype(held_as)


def setup_inputs(seed: int = 0) -> dict:
    seeds = jax.random.split(jax.random.key(seed), 6)
    return {
        "fiber_rows": bell_draw(seeds[0], (FIBERS, RR), 1.0, 6.0, ((0, 32),)),
        "fiber_i": draw_fiber_i(jax.random.fold_in(seeds[5], 71), 0),
        "fiber_j": draw_fiber_j(jax.random.fold_in(seeds[5], 71), 0),
        "fiber_count": draw_fiber_count(jax.random.fold_in(seeds[5], 71), 0),
        "factor_two": bell_draw(seeds[4], (I2, R), 0.15, 1.0, ((0, 8),)),
    }


def reference(fiber_rows, fiber_i, fiber_j, fiber_count, factor_two):
    slot_ids = jnp.arange(FIBERS, dtype=jnp.int32)
    owners = slot_ids // FIB_DEV
    live = (slot_ids % FIB_DEV) < fiber_count[owners]
    target = jnp.where(live, fiber_i, I1).astype(jnp.int32)
    factor_rows = factor_two[fiber_j]
    block = min(512, FIBERS)
    nblocks = FIBERS // block
    rows_blocks = fiber_rows.reshape(nblocks, block, RR)
    factor_blocks = factor_rows.reshape(nblocks, block, R)
    target_blocks = target.reshape(nblocks, block)

    def accumulate(total, pieces):
        rows, factors, targets = pieces
        outer = factors.astype(jnp.float32)[:, :, None] * rows.astype(jnp.float32)[:, None, :]
        total = total.at[targets].add(outer.reshape(block, R * RR), mode="drop")
        return total, None

    start = jnp.zeros((I1, R * RR), jnp.float32)
    total, _ = lax.scan(accumulate, start, (rows_blocks, factor_blocks, target_blocks))
    return total.astype(jnp.bfloat16)
```

```python
import functools

import jax
import jax.numpy as jnp
from jax import lax
from jax.experimental import pallas as pl
from jax.experimental.pallas import tpu as pltpu
from jax.sharding import PartitionSpec as P

I_DEV = 128
LANES = 128
KBLOCK = 256
MESH = pl.DeviceIdType.MESH
ORDER = (1, 2, 3, 0)


def contract_lanes(a, b):
    return lax.dot_general(a, b, (((1,), (1,)), ((), ())), preferred_element_type=jnp.float32)


def pack_kernel(
    n, cap, halves, steps, count_ref, i_ref, j_ref, rows_ref, factor_ref, out_ref, meta_ref, slot_ref
):
    stored = rows_ref.shape[0]
    rank, col_rows = factor_ref.shape
    block = out_ref.shape[0]
    step = pl.program_id(0)

    @pl.when(step == 0)
    def _():
        index = i_ref[...]
        shift = I_DEV.bit_length() - 1
        target = jnp.right_shift(index, shift)
        local_i = jnp.bitwise_and(index, I_DEV - 1)
        live = lax.broadcasted_iota(jnp.int32, (1, stored), 1) < count_ref[0]
        target = jnp.where(live, target, -1)
        member = lax.broadcasted_iota(jnp.int32, (n, stored), 0) == target
        earlier = lax.broadcasted_iota(jnp.int32, (stored, stored), 0) < lax.broadcasted_iota(
            jnp.int32, (stored, stored), 1
        )
        before = jnp.dot(
            member.astype(jnp.float32).astype(jnp.bfloat16),
            earlier.astype(jnp.float32).astype(jnp.bfloat16),
            preferred_element_type=jnp.float32,
        )
        position = jnp.sum(jnp.where(member, before, 0.0), axis=0, keepdims=True).astype(jnp.int32)
        slot_ref[...] = jnp.where(live, target * cap + position, -1)

        local_j = j_ref[...] - lax.axis_index("col") * col_rows
        high = jnp.right_shift(local_j, KBLOCK.bit_length() - 1)
        low = jnp.bitwise_and(local_j, KBLOCK - 1)
        chosen = lax.broadcasted_iota(jnp.int32, (KBLOCK, stored), 0) == low
        chosen = chosen.astype(jnp.float32).astype(jnp.bfloat16)
        pieces = col_rows // KBLOCK
        stacked = jnp.concatenate(
            [factor_ref[:, k * KBLOCK : (k + 1) * KBLOCK] for k in range(pieces)], axis=0
        )
        looked = jnp.dot(stacked, chosen, preferred_element_type=jnp.float32)
        own = jnp.zeros((rank, stored), jnp.float32)
        for k in range(pieces):
            own = own + jnp.where(high == k, looked[k * rank : (k + 1) * rank], 0.0)

        hc = cap // halves
        part = LANES // halves
        half = jnp.zeros_like(position)
        for h in range(1, halves):
            half = half + (position >= h * hc).astype(jnp.int32)
        half_slot = jnp.where(live, target * hc + position - half * hc, -1)
        place = jnp.broadcast_to(local_i.astype(jnp.float32), (8, stored))
        filler = jnp.zeros((part - rank - 8, stored), jnp.float32)
        chunks = []
        for h in range(halves):
            chunk = jnp.concatenate([own, place, filler], axis=0)
            chunks.append(jnp.where(half == h, chunk, 0.0))
        table = jnp.concatenate(chunks, axis=0).astype(jnp.bfloat16)
        spread = lax.broadcasted_iota(jnp.int32, (n * hc, stored), 0) == half_slot
        spread = spread.astype(jnp.float32).astype(jnp.bfloat16)
        meta_ref[...] = contract_lanes(spread, table).astype(jnp.bfloat16)

    ids = lax.broadcasted_iota(jnp.int32, (block, stored), 0) + step * block
    move = (ids == slot_ref[...]).astype(jnp.float32).astype(jnp.bfloat16)
    out_ref[...] = jnp.dot(move, rows_ref[...], preferred_element_type=jnp.float32).astype(
        jnp.bfloat16
    )


def flip(z, g, groups):
    out = 0
    bit = 1
    while bit < groups:
        out = out + bit * ((z // bit + g // bit) % 2)
        bit *= 2
    return out


def exchange_kernel(
    nrow, ncol, groups, rows_ref, meta_ref, rrows_ref, rmeta_ref, send_sem, recv_sem, own_sem
):
    n = nrow * ncol
    members = n // groups
    per = ncol // groups
    r = lax.axis_index("row")
    c = lax.axis_index("col")
    me = r * ncol + c
    z, y = c // per, c % per
    seat = r * per + y

    barrier = pltpu.get_barrier_semaphore()

    def greet(k, _):
        other = (me + k) % n
        pl.semaphore_signal(
            barrier, inc=1, device_id=(other // ncol, other % ncol), device_id_type=MESH
        )
        return 0

    lax.fori_loop(1, n, greet, 0)
    own_rows = pltpu.make_async_copy(rows_ref.at[me], rrows_ref.at[0, :, seat], own_sem.at[0])
    own_meta = pltpu.make_async_copy(meta_ref.at[me], rmeta_ref.at[0, seat], own_sem.at[1])
    own_rows.start()
    own_meta.start()
    pl.semaphore_wait(barrier, n - 1)

    def copies(g, k):
        tr = (r + k // per) % nrow
        tc = flip(z, g, groups) * per + (y + k % per) % per
        other = tr * ncol + tc
        t = g * members + k
        return (
            pltpu.make_async_remote_copy(
                src_ref=rows_ref.at[other],
                dst_ref=rrows_ref.at[g, :, seat],
                send_sem=send_sem.at[0, t],
                recv_sem=recv_sem.at[0, t],
                device_id=(tr, tc),
                device_id_type=MESH,
            ),
            pltpu.make_async_remote_copy(
                src_ref=meta_ref.at[other],
                dst_ref=rmeta_ref.at[g, seat],
                send_sem=send_sem.at[1, t],
                recv_sem=recv_sem.at[1, t],
                device_id=(tr, tc),
                device_id_type=MESH,
            ),
        )

    for g in ORDER:
        def send(k, _, g=g):
            for copy in copies(g, k):
                copy.start()
            return 0

        lax.fori_loop(1 if g == 0 else 0, members, send, 0)
    for g in ORDER:
        def finish(k, _, g=g):
            for copy in copies(g, k):
                copy.wait_recv()
                copy.wait_send()
            return 0

        lax.fori_loop(1 if g == 0 else 0, members, finish, 0)
    own_rows.wait()
    own_meta.wait()


def contract_kernel(groups, halves, rows_ref, meta_ref, out_ref, factor_ref, select_ref):
    slots, width = rows_ref.shape
    rank = factor_ref.shape[0]
    kgroup = slots // groups
    part = LANES // halves
    span = kgroup // halves
    per = out_ref.shape[1] // width
    step = pl.program_id(0)

    @pl.when(step == 0)
    def _():
        for g in range(groups):
            turned = meta_ref[g * span : (g + 1) * span, :].astype(jnp.float32).T
            for h in range(halves):
                first = g * kgroup + h * span
                factor_ref[:, first : first + span] = turned[h * part : h * part + rank]
                place = turned[h * part + rank : h * part + rank + 1]
                owned = lax.broadcasted_iota(jnp.int32, (I_DEV, span), 0).astype(jnp.float32)
                select_ref[:, first : first + span] = (
                    (owned == place).astype(jnp.float32).astype(jnp.bfloat16)
                )

    select = select_ref[...]
    left = jnp.concatenate(
        [select * factor_ref[pl.ds(step * per + b, 1), :].astype(jnp.bfloat16) for b in range(per)],
        axis=0,
    )
    total = jnp.dot(left, rows_ref[...], preferred_element_type=jnp.float32)
    for b in range(per):
        out_ref[:, b * width : (b + 1) * width] = total[b * I_DEV : (b + 1) * I_DEV].astype(
            jnp.bfloat16
        )


def body(nrow, ncol, fiber_rows, fiber_i, fiber_j, fiber_count, factor_two):
    n = nrow * ncol
    stored, width = fiber_rows.shape
    col_rows, rank = factor_two.shape
    cap = 2 * stored // n
    slots = n * cap
    halves = 2 if cap % 32 == 0 else 1
    hc = cap // halves
    groups = slots // KBLOCK
    members = n // groups
    steps = 4
    whole = lambda s: (0, 0)
    vmem = 60 * 1024 * 1024
    packed, meta = pl.pallas_call(
        functools.partial(pack_kernel, n, cap, halves, steps),
        out_shape=(
            jax.ShapeDtypeStruct((slots, width), jnp.bfloat16),
            jax.ShapeDtypeStruct((n * hc, LANES), jnp.bfloat16),
        ),
        grid=(steps,),
        in_specs=[
            pl.BlockSpec(memory_space=pltpu.SMEM),
            pl.BlockSpec((1, stored), whole),
            pl.BlockSpec((1, stored), whole),
            pl.BlockSpec((stored, width), whole),
            pl.BlockSpec((rank, col_rows), whole),
        ],
        out_specs=(
            pl.BlockSpec((slots // steps, width), lambda s: (s, 0)),
            pl.BlockSpec((n * hc, LANES), whole),
        ),
        scratch_shapes=[pltpu.VMEM((1, stored), jnp.int32)],
        name="pack",
    )(
        fiber_count,
        fiber_i.reshape(1, stored),
        fiber_j.reshape(1, stored),
        fiber_rows,
        factor_two.T,
    )
    got_rows, got_meta = pl.pallas_call(
        functools.partial(exchange_kernel, nrow, ncol, groups),
        out_shape=(
            jax.ShapeDtypeStruct((groups, halves, members, hc, width), jnp.bfloat16),
            jax.ShapeDtypeStruct((groups, members, hc, LANES), jnp.bfloat16),
        ),
        in_specs=[pl.BlockSpec(memory_space=pl.ANY)] * 2,
        out_specs=(pl.BlockSpec(memory_space=pl.ANY),) * 2,
        scratch_shapes=[
            pltpu.SemaphoreType.DMA((2, n)),
            pltpu.SemaphoreType.DMA((2, n)),
            pltpu.SemaphoreType.DMA((2,)),
        ],
        compiler_params=pltpu.CompilerParams(collective_id=0, has_side_effects=True),
        name="exchange",
    )(packed.reshape(n, halves, hc, width), meta.reshape(n, hc, LANES))
    per = 4
    return pl.pallas_call(
        functools.partial(contract_kernel, groups, halves),
        out_shape=jax.ShapeDtypeStruct((I_DEV, rank * width), jnp.bfloat16),
        grid=(rank // per,),
        in_specs=[
            pl.BlockSpec((slots, width), whole),
            pl.BlockSpec((n * hc, LANES), whole),
        ],
        out_specs=pl.BlockSpec((I_DEV, per * width), lambda s: (0, s)),
        scratch_shapes=[
            pltpu.VMEM((rank, slots), jnp.float32),
            pltpu.VMEM((I_DEV, slots), jnp.bfloat16),
        ],
        name="contract",
    )(got_rows.reshape(slots, width), got_meta.reshape(n * hc, LANES))


def solution(mesh):
    in_specs = (
        P(("row", "col"), None),
        P(("row", "col")),
        P(("row", "col")),
        P(("row", "col")),
        P("col", None),
    )
    out_specs = P(("row", "col"), None)
    step = functools.partial(body, mesh.shape["row"], mesh.shape["col"])
    return jax.shard_map(step, mesh=mesh, in_specs=in_specs, out_specs=out_specs, check_vma=False)
```

```python
import functools

import jax
import jax.numpy as jnp
from jax import lax
from jax.experimental import pallas as pl
from jax.experimental.pallas import tpu as pltpu
from jax.sharding import PartitionSpec as P

I_DEV = 128
LANES = 128
KBLOCK = 256
MESH = pl.DeviceIdType.MESH
ORDER = (1, 2, 3, 0)
ARRIVAL = (0, 1, 2, 3)


def contract_lanes(a, b):
    return lax.dot_general(a, b, (((1,), (1,)), ((), ())), preferred_element_type=jnp.float32)


def pack_kernel(
    n, cap, halves, steps, count_ref, i_ref, j_ref, rows_ref, factor_ref, out_ref, meta_ref, slot_ref
):
    stored = rows_ref.shape[0]
    rank, col_rows = factor_ref.shape
    block = out_ref.shape[0]
    step = pl.program_id(0)

    @pl.when(step == 0)
    def _():
        index = i_ref[...]
        shift = I_DEV.bit_length() - 1
        target = jnp.right_shift(index, shift)
        local_i = jnp.bitwise_and(index, I_DEV - 1)
        live = lax.broadcasted_iota(jnp.int32, (1, stored), 1) < count_ref[0]
        target = jnp.where(live, target, -1)
        member = lax.broadcasted_iota(jnp.int32, (n, stored), 0) == target
        earlier = lax.broadcasted_iota(jnp.int32, (stored, stored), 0) < lax.broadcasted_iota(
            jnp.int32, (stored, stored), 1
        )
        before = jnp.dot(
            member.astype(jnp.float32).astype(jnp.bfloat16),
            earlier.astype(jnp.float32).astype(jnp.bfloat16),
            preferred_element_type=jnp.float32,
        )
        position = jnp.sum(jnp.where(member, before, 0.0), axis=0, keepdims=True).astype(jnp.int32)
        slot_ref[...] = jnp.where(live, target * cap + position, -1)

        local_j = j_ref[...] - lax.axis_index("col") * col_rows
        high = jnp.right_shift(local_j, KBLOCK.bit_length() - 1)
        low = jnp.bitwise_and(local_j, KBLOCK - 1)
        chosen = lax.broadcasted_iota(jnp.int32, (KBLOCK, stored), 0) == low
        chosen = chosen.astype(jnp.float32).astype(jnp.bfloat16)
        pieces = col_rows // KBLOCK
        stacked = jnp.concatenate(
            [factor_ref[:, k * KBLOCK : (k + 1) * KBLOCK] for k in range(pieces)], axis=0
        )
        looked = jnp.dot(stacked, chosen, preferred_element_type=jnp.float32)
        own = jnp.zeros((rank, stored), jnp.float32)
        for k in range(pieces):
            own = own + jnp.where(high == k, looked[k * rank : (k + 1) * rank], 0.0)

        hc = cap // halves
        part = LANES // halves
        half = jnp.zeros_like(position)
        for h in range(1, halves):
            half = half + (position >= h * hc).astype(jnp.int32)
        half_slot = jnp.where(live, target * hc + position - half * hc, -1)
        place = jnp.broadcast_to(local_i.astype(jnp.float32), (8, stored))
        filler = jnp.zeros((part - rank - 8, stored), jnp.float32)
        chunks = []
        for h in range(halves):
            chunk = jnp.concatenate([own, place, filler], axis=0)
            chunks.append(jnp.where(half == h, chunk, 0.0))
        table = jnp.concatenate(chunks, axis=0).astype(jnp.bfloat16)
        spread = lax.broadcasted_iota(jnp.int32, (n * hc, stored), 0) == half_slot
        spread = spread.astype(jnp.float32).astype(jnp.bfloat16)
        meta_ref[...] = contract_lanes(spread, table).astype(jnp.bfloat16)

    ids = lax.broadcasted_iota(jnp.int32, (block, stored), 0) + step * block
    move = (ids == slot_ref[...]).astype(jnp.float32).astype(jnp.bfloat16)
    out_ref[...] = jnp.dot(move, rows_ref[...], preferred_element_type=jnp.float32).astype(
        jnp.bfloat16
    )


def flip(z, g, groups):
    out = 0
    bit = 1
    while bit < groups:
        out = out + bit * ((z // bit + g // bit) % 2)
        bit *= 2
    return out


def expand(meta, halves, factor_ref, select_ref):
    span = meta.shape[0]
    rank = factor_ref.shape[0]
    part = LANES // halves
    turned = meta.astype(jnp.float32).T
    for h in range(halves):
        first = h * span
        factor_ref[:, first : first + span] = turned[h * part : h * part + rank]
        place = turned[h * part + rank : h * part + rank + 1]
        owned = lax.broadcasted_iota(jnp.int32, (I_DEV, span), 0).astype(jnp.float32)
        select_ref[:, first : first + span] = (
            (owned == place).astype(jnp.float32).astype(jnp.bfloat16)
        )


def spread_factors(select, factor_ref, first, count):
    return jnp.concatenate(
        [
            select * factor_ref[pl.ds(first + b, 1), :].astype(jnp.bfloat16)
            for b in range(count)
        ],
        axis=0,
    )


def exchange_kernel(
    nrow,
    ncol,
    groups,
    halves,
    rows_ref,
    meta_ref,
    rrows_ref,
    rmeta_ref,
    total_ref,
    factor_ref,
    select_ref,
    send_sem,
    recv_sem,
    own_sem,
):
    n = nrow * ncol
    members = n // groups
    per = ncol // groups
    r = lax.axis_index("row")
    c = lax.axis_index("col")
    me = r * ncol + c
    z, y = c // per, c % per
    seat = r * per + y

    barrier = pltpu.get_barrier_semaphore()

    def greet(k, _):
        other = (me + k) % n
        pl.semaphore_signal(
            barrier, inc=1, device_id=(other // ncol, other % ncol), device_id_type=MESH
        )
        return 0

    lax.fori_loop(1, n, greet, 0)
    own_rows = pltpu.make_async_copy(rows_ref.at[me], rrows_ref.at[0, :, seat], own_sem.at[0])
    own_meta = pltpu.make_async_copy(meta_ref.at[me], rmeta_ref.at[0, seat], own_sem.at[1])
    own_rows.start()
    own_meta.start()
    pl.semaphore_wait(barrier, n - 1)

    def copies(g, k):
        tr = (r + k // per) % nrow
        tc = flip(z, g, groups) * per + (y + k % per) % per
        other = tr * ncol + tc
        t = g * members + k
        return (
            pltpu.make_async_remote_copy(
                src_ref=rows_ref.at[other],
                dst_ref=rrows_ref.at[g, :, seat],
                send_sem=send_sem.at[0, t],
                recv_sem=recv_sem.at[0, t],
                device_id=(tr, tc),
                device_id_type=MESH,
            ),
            pltpu.make_async_remote_copy(
                src_ref=meta_ref.at[other],
                dst_ref=rmeta_ref.at[g, seat],
                send_sem=send_sem.at[1, t],
                recv_sem=recv_sem.at[1, t],
                device_id=(tr, tc),
                device_id_type=MESH,
            ),
        )

    for g in ORDER:
        def send(k, _, g=g):
            for copy in copies(g, k):
                copy.start()
            return 0

        lax.fori_loop(1 if g == 0 else 0, members, send, 0)
    rank = factor_ref.shape[0]
    width = total_ref.shape[1]
    span = rmeta_ref.shape[1] * rmeta_ref.shape[2]
    kgroup = span * halves
    per_step = 8

    for place_in_order, g in enumerate(ARRIVAL):
        def arrive(k, _, g=g):
            for copy in copies(g, k):
                copy.wait_recv()
            return 0

        lax.fori_loop(1 if g == 0 else 0, members, arrive, 0)
        if g == 0:
            own_rows.wait()
            own_meta.wait()
        if place_in_order == groups - 1:
            break
        expand(rmeta_ref[g].reshape(span, LANES), halves, factor_ref, select_ref)

        def multiply(s, _, g=g, place_in_order=place_in_order):
            select = select_ref[...]
            left = spread_factors(select, factor_ref, s * per_step, per_step)
            product = jnp.dot(
                left, rrows_ref[g].reshape(kgroup, width), preferred_element_type=jnp.float32
            )
            span_m = per_step * I_DEV
            rows = pl.ds(pl.multiple_of(s * span_m, span_m), span_m)
            if place_in_order > 0:
                product = product + total_ref[rows, :]
            total_ref[rows, :] = product
            return 0

        lax.fori_loop(0, rank // per_step, multiply, 0)

    for g in ORDER:
        def finish(k, _, g=g):
            for copy in copies(g, k):
                copy.wait_send()
            return 0

        lax.fori_loop(1 if g == 0 else 0, members, finish, 0)


def contract_kernel(
    halves, rows_ref, meta_ref, total_ref, out_ref, stage_ref, factor_ref, select_ref, sem
):
    last = ARRIVAL[-1]
    rank, kgroup = factor_ref.shape
    width = total_ref.shape[1]
    per = stage_ref.shape[2] // width
    steps = rank // per
    expand(meta_ref[last].reshape(kgroup // halves, LANES), halves, factor_ref, select_ref)

    def copy_out(s, slot):
        at = pl.multiple_of(s * per * width, per * width)
        return pltpu.make_async_copy(
            stage_ref.at[slot], out_ref.at[:, pl.ds(at, per * width)], sem.at[slot]
        )

    def multiply(s, _):
        slot = s % 2

        @pl.when(s >= 2)
        def _():
            copy_out(s - 2, slot).wait()

        left = spread_factors(select_ref[...], factor_ref, s * per, per)
        product = jnp.dot(
            left, rows_ref[last].reshape(kgroup, width), preferred_element_type=jnp.float32
        )
        span_m = per * I_DEV
        product = product + total_ref[pl.ds(pl.multiple_of(s * span_m, span_m), span_m), :]
        for b in range(per):
            stage_ref[slot, :, b * width : (b + 1) * width] = product[
                b * I_DEV : (b + 1) * I_DEV
            ].astype(jnp.bfloat16)
        copy_out(s, slot).start()
        return 0

    lax.fori_loop(0, steps, multiply, 0)
    copy_out(steps - 2, steps % 2).wait()
    copy_out(steps - 1, (steps - 1) % 2).wait()


def body(nrow, ncol, fiber_rows, fiber_i, fiber_j, fiber_count, factor_two):
    n = nrow * ncol
    stored, width = fiber_rows.shape
    col_rows, rank = factor_two.shape
    cap = 2 * stored // n
    slots = n * cap
    halves = 2 if cap % 32 == 0 else 1
    hc = cap // halves
    groups = slots // KBLOCK
    members = n // groups
    steps = 4
    whole = lambda s: (0, 0)
    packed, meta = pl.pallas_call(
        functools.partial(pack_kernel, n, cap, halves, steps),
        out_shape=(
            jax.ShapeDtypeStruct((slots, width), jnp.bfloat16),
            jax.ShapeDtypeStruct((n * hc, LANES), jnp.bfloat16),
        ),
        grid=(steps,),
        in_specs=[
            pl.BlockSpec(memory_space=pltpu.SMEM),
            pl.BlockSpec((1, stored), whole),
            pl.BlockSpec((1, stored), whole),
            pl.BlockSpec((stored, width), whole),
            pl.BlockSpec((rank, col_rows), whole),
        ],
        out_specs=(
            pl.BlockSpec((slots // steps, width), lambda s: (s, 0)),
            pl.BlockSpec((n * hc, LANES), whole),
        ),
        scratch_shapes=[pltpu.VMEM((1, stored), jnp.int32)],
        name="pack",
    )(
        fiber_count,
        fiber_i.reshape(1, stored),
        fiber_j.reshape(1, stored),
        fiber_rows,
        factor_two.T,
    )
    in_vmem = pl.BlockSpec(memory_space=pltpu.VMEM)
    got_rows, got_meta, total = pl.pallas_call(
        functools.partial(exchange_kernel, nrow, ncol, groups, halves),
        out_shape=(
            jax.ShapeDtypeStruct((groups, halves, members, hc, width), jnp.bfloat16),
            jax.ShapeDtypeStruct((groups, members, hc, LANES), jnp.bfloat16),
            jax.ShapeDtypeStruct((I_DEV * rank, width), jnp.float32),
        ),
        in_specs=[pl.BlockSpec(memory_space=pl.ANY)] * 2,
        out_specs=(in_vmem, in_vmem, in_vmem),
        scratch_shapes=[
            pltpu.VMEM((rank, KBLOCK), jnp.float32),
            pltpu.VMEM((I_DEV, KBLOCK), jnp.bfloat16),
            pltpu.SemaphoreType.DMA((2, n)),
            pltpu.SemaphoreType.DMA((2, n)),
            pltpu.SemaphoreType.DMA((2,)),
        ],
        compiler_params=pltpu.CompilerParams(
            collective_id=0, has_side_effects=True, vmem_limit_bytes=24 * 1024 * 1024
        ),
        name="exchange",
    )(packed.reshape(n, halves, hc, width), meta.reshape(n, hc, LANES))
    per = 4
    return pl.pallas_call(
        functools.partial(contract_kernel, halves),
        out_shape=jax.ShapeDtypeStruct((I_DEV, rank * width), jnp.bfloat16),
        in_specs=[in_vmem, in_vmem, in_vmem],
        out_specs=pl.BlockSpec(memory_space=pl.ANY),
        scratch_shapes=[
            pltpu.VMEM((2, I_DEV, per * width), jnp.bfloat16),
            pltpu.VMEM((rank, KBLOCK), jnp.float32),
            pltpu.VMEM((I_DEV, KBLOCK), jnp.bfloat16),
            pltpu.SemaphoreType.DMA((2,)),
        ],
        compiler_params=pltpu.CompilerParams(vmem_limit_bytes=24 * 1024 * 1024),
        name="contract",
    )(got_rows, got_meta, total)


def solution(mesh):
    in_specs = (
        P(("row", "col"), None),
        P(("row", "col")),
        P(("row", "col")),
        P(("row", "col")),
        P("col", None),
    )
    out_specs = P(("row", "col"), None)
    step = functools.partial(body, mesh.shape["row"], mesh.shape["col"])
    return jax.shard_map(step, mesh=mesh, in_specs=in_specs, out_specs=out_specs, check_vma=False)
```

```python
import functools

import jax
import jax.numpy as jnp
from jax import lax
from jax.experimental import pallas as pl
from jax.experimental.pallas import tpu as pltpu
from jax.sharding import PartitionSpec as P

I_DEV = 128
LANES = 128
KBLOCK = 256
MESH = pl.DeviceIdType.MESH
ORDER = (1, 2, 3, 0)
ARRIVAL = (0, 1, 2, 3)


def contract_lanes(a, b):
    return lax.dot_general(a, b, (((1,), (1,)), ((), ())), preferred_element_type=jnp.float32)


def pack(
    n, cap, halves, count_ref, i_ref, j_ref, rows_ref, factor_ref, out_ref, meta_ref, ready
):
    stored = rows_ref.shape[0]
    rank, col_rows = factor_ref.shape
    for copy in ready[:3]:
        copy.wait()
    index = i_ref[...]
    shift = I_DEV.bit_length() - 1
    target = jnp.right_shift(index, shift)
    local_i = jnp.bitwise_and(index, I_DEV - 1)
    live = lax.broadcasted_iota(jnp.int32, (1, stored), 1) < count_ref[0]
    target = jnp.where(live, target, -1)
    member = lax.broadcasted_iota(jnp.int32, (n, stored), 0) == target
    earlier = lax.broadcasted_iota(jnp.int32, (stored, stored), 0) < lax.broadcasted_iota(
        jnp.int32, (stored, stored), 1
    )
    before = jnp.dot(
        member.astype(jnp.float32).astype(jnp.bfloat16),
        earlier.astype(jnp.float32).astype(jnp.bfloat16),
        preferred_element_type=jnp.float32,
    )
    position = jnp.sum(jnp.where(member, before, 0.0), axis=0, keepdims=True).astype(jnp.int32)
    slot = jnp.where(live, target * cap + position, -1)

    local_j = j_ref[...] - lax.axis_index("col") * col_rows
    high = jnp.right_shift(local_j, KBLOCK.bit_length() - 1)
    low = jnp.bitwise_and(local_j, KBLOCK - 1)
    chosen = lax.broadcasted_iota(jnp.int32, (KBLOCK, stored), 0) == low
    chosen = chosen.astype(jnp.float32).astype(jnp.bfloat16)
    pieces = col_rows // KBLOCK
    stacked = jnp.concatenate(
        [factor_ref[:, k * KBLOCK : (k + 1) * KBLOCK] for k in range(pieces)], axis=0
    )
    looked = jnp.dot(stacked, chosen, preferred_element_type=jnp.float32)
    own = jnp.zeros((rank, stored), jnp.float32)
    for k in range(pieces):
        own = own + jnp.where(high == k, looked[k * rank : (k + 1) * rank], 0.0)

    hc = cap // halves
    part = LANES // halves
    half = jnp.zeros_like(position)
    for h in range(1, halves):
        half = half + (position >= h * hc).astype(jnp.int32)
    half_slot = jnp.where(live, target * hc + position - half * hc, -1)
    place = jnp.broadcast_to(local_i.astype(jnp.float32), (8, stored))
    filler = jnp.zeros((part - rank - 8, stored), jnp.float32)
    chunks = []
    for h in range(halves):
        chunk = jnp.concatenate([own, place, filler], axis=0)
        chunks.append(jnp.where(half == h, chunk, 0.0))
    table = jnp.concatenate(chunks, axis=0).astype(jnp.bfloat16)
    spread = lax.broadcasted_iota(jnp.int32, (n * hc, stored), 0) == half_slot
    spread = spread.astype(jnp.float32).astype(jnp.bfloat16)
    meta_ref[...] = contract_lanes(spread, table).astype(jnp.bfloat16).reshape(meta_ref.shape)

    ready[3].wait()
    fiber_rows = rows_ref[...]
    targets = KBLOCK // cap
    for step in range(n // targets):
        ids = lax.broadcasted_iota(jnp.int32, (KBLOCK, stored), 0) + step * KBLOCK
        move = (ids == slot).astype(jnp.float32).astype(jnp.bfloat16)
        moved = jnp.dot(move, fiber_rows, preferred_element_type=jnp.float32).astype(jnp.bfloat16)
        out_ref[step * targets : (step + 1) * targets] = moved.reshape(
            (targets,) + out_ref.shape[1:]
        )


def flip(z, g, groups):
    out = 0
    bit = 1
    while bit < groups:
        out = out + bit * ((z // bit + g // bit) % 2)
        bit *= 2
    return out


def expand(meta, halves, factor_ref, select_ref):
    span = meta.shape[0]
    rank = factor_ref.shape[0]
    part = LANES // halves
    turned = meta.astype(jnp.float32).T
    for h in range(halves):
        first = h * span
        factor_ref[:, first : first + span] = turned[h * part : h * part + rank]
        place = turned[h * part + rank : h * part + rank + 1]
        owned = lax.broadcasted_iota(jnp.int32, (I_DEV, span), 0).astype(jnp.float32)
        select_ref[:, first : first + span] = (
            (owned == place).astype(jnp.float32).astype(jnp.bfloat16)
        )


def spread_factors(select, factor_ref, first, count):
    return jnp.concatenate(
        [
            select * factor_ref[pl.ds(first + b, 1), :].astype(jnp.bfloat16)
            for b in range(count)
        ],
        axis=0,
    )


def exchange_kernel(
    nrow,
    ncol,
    groups,
    halves,
    count_ref,
    i_hbm,
    j_hbm,
    fiber_hbm,
    factor_hbm,
    rrows_ref,
    rmeta_ref,
    total_ref,
    i_ref,
    j_ref,
    fiber_ref,
    own_factor_ref,
    rows_ref,
    meta_ref,
    factor_ref,
    select_ref,
    send_sem,
    recv_sem,
    own_sem,
    in_sem,
):
    n = nrow * ncol
    members = n // groups
    per = ncol // groups
    r = lax.axis_index("row")
    c = lax.axis_index("col")
    me = r * ncol + c
    z, y = c // per, c % per
    seat = r * per + y

    barrier = pltpu.get_barrier_semaphore()

    def greet(k, _):
        other = (me + k) % n
        pl.semaphore_signal(
            barrier, inc=1, device_id=(other // ncol, other % ncol), device_id_type=MESH
        )
        return 0

    ready = (
        pltpu.make_async_copy(i_hbm, i_ref, in_sem.at[0]),
        pltpu.make_async_copy(j_hbm, j_ref, in_sem.at[1]),
        pltpu.make_async_copy(factor_hbm, own_factor_ref, in_sem.at[2]),
        pltpu.make_async_copy(fiber_hbm, fiber_ref, in_sem.at[3]),
    )
    for copy in ready:
        copy.start()
    lax.fori_loop(1, n, greet, 0)
    pack(
        n,
        halves * rows_ref.shape[2],
        halves,
        count_ref,
        i_ref,
        j_ref,
        fiber_ref,
        own_factor_ref,
        rows_ref,
        meta_ref,
        ready,
    )
    pl.semaphore_wait(barrier, n - 1)
    own_rows = pltpu.make_async_copy(rows_ref.at[me], rrows_ref.at[0, :, seat], own_sem.at[0])
    own_meta = pltpu.make_async_copy(meta_ref.at[me], rmeta_ref.at[0, seat], own_sem.at[1])

    def copies(g, k):
        tr = (r + k // per) % nrow
        tc = flip(z, g, groups) * per + (y + k % per) % per
        other = tr * ncol + tc
        t = g * members + k
        return (
            pltpu.make_async_remote_copy(
                src_ref=rows_ref.at[other],
                dst_ref=rrows_ref.at[g, :, seat],
                send_sem=send_sem.at[0, t],
                recv_sem=recv_sem.at[0, t],
                device_id=(tr, tc),
                device_id_type=MESH,
            ),
            pltpu.make_async_remote_copy(
                src_ref=meta_ref.at[other],
                dst_ref=rmeta_ref.at[g, seat],
                send_sem=send_sem.at[1, t],
                recv_sem=recv_sem.at[1, t],
                device_id=(tr, tc),
                device_id_type=MESH,
            ),
        )

    for g in ORDER:
        def send(k, _, g=g):
            for copy in copies(g, k):
                copy.start()
            return 0

        lax.fori_loop(1 if g == 0 else 0, members, send, 0)
    own_rows.start()
    own_meta.start()
    rank = factor_ref.shape[0]
    width = total_ref.shape[1]
    span = rmeta_ref.shape[1] * rmeta_ref.shape[2]
    kgroup = span * halves
    per_step = 8

    for place_in_order, g in enumerate(ARRIVAL):
        def arrive(k, _, g=g):
            for copy in copies(g, k):
                copy.wait_recv()
            return 0

        lax.fori_loop(1 if g == 0 else 0, members, arrive, 0)
        if g == 0:
            own_rows.wait()
            own_meta.wait()
        if place_in_order == groups - 1:
            break
        expand(rmeta_ref[g].reshape(span, LANES), halves, factor_ref, select_ref)

        def multiply(s, _, g=g, place_in_order=place_in_order):
            select = select_ref[...]
            left = spread_factors(select, factor_ref, s * per_step, per_step)
            product = jnp.dot(
                left, rrows_ref[g].reshape(kgroup, width), preferred_element_type=jnp.float32
            )
            span_m = per_step * I_DEV
            rows = pl.ds(pl.multiple_of(s * span_m, span_m), span_m)
            if place_in_order > 0:
                product = product + total_ref[rows, :]
            total_ref[rows, :] = product
            return 0

        lax.fori_loop(0, rank // per_step, multiply, 0)

    for g in ORDER:
        def finish(k, _, g=g):
            for copy in copies(g, k):
                copy.wait_send()
            return 0

        lax.fori_loop(1 if g == 0 else 0, members, finish, 0)


def contract_kernel(
    halves, rows_ref, meta_ref, total_ref, out_ref, stage_ref, factor_ref, select_ref, sem
):
    last = ARRIVAL[-1]
    rank, kgroup = factor_ref.shape
    width = total_ref.shape[1]
    per = stage_ref.shape[2] // width
    steps = rank // per
    expand(meta_ref[last].reshape(kgroup // halves, LANES), halves, factor_ref, select_ref)

    def copy_out(s, slot):
        at = pl.multiple_of(s * per * width, per * width)
        return pltpu.make_async_copy(
            stage_ref.at[slot], out_ref.at[:, pl.ds(at, per * width)], sem.at[slot]
        )

    def multiply(s, _):
        slot = s % 2

        @pl.when(s >= 2)
        def _():
            copy_out(s - 2, slot).wait()

        left = spread_factors(select_ref[...], factor_ref, s * per, per)
        product = jnp.dot(
            left, rows_ref[last].reshape(kgroup, width), preferred_element_type=jnp.float32
        )
        span_m = per * I_DEV
        product = product + total_ref[pl.ds(pl.multiple_of(s * span_m, span_m), span_m), :]
        for b in range(per):
            stage_ref[slot, :, b * width : (b + 1) * width] = product[
                b * I_DEV : (b + 1) * I_DEV
            ].astype(jnp.bfloat16)
        copy_out(s, slot).start()
        return 0

    lax.fori_loop(0, steps, multiply, 0)
    copy_out(steps - 2, steps % 2).wait()
    copy_out(steps - 1, (steps - 1) % 2).wait()


def body(nrow, ncol, fiber_rows, fiber_i, fiber_j, fiber_count, factor_two):
    n = nrow * ncol
    stored, width = fiber_rows.shape
    col_rows, rank = factor_two.shape
    cap = 2 * stored // n
    slots = n * cap
    halves = 2 if cap % 32 == 0 else 1
    hc = cap // halves
    groups = slots // KBLOCK
    members = n // groups
    in_vmem = pl.BlockSpec(memory_space=pltpu.VMEM)
    got_rows, got_meta, total = pl.pallas_call(
        functools.partial(exchange_kernel, nrow, ncol, groups, halves),
        out_shape=(
            jax.ShapeDtypeStruct((groups, halves, members, hc, width), jnp.bfloat16),
            jax.ShapeDtypeStruct((groups, members, hc, LANES), jnp.bfloat16),
            jax.ShapeDtypeStruct((I_DEV * rank, width), jnp.float32),
        ),
        in_specs=[pl.BlockSpec(memory_space=pltpu.SMEM)] + [pl.BlockSpec(memory_space=pltpu.HBM)] * 4,
        out_specs=(in_vmem, in_vmem, in_vmem),
        scratch_shapes=[
            pltpu.VMEM((1, stored), jnp.int32),
            pltpu.VMEM((1, stored), jnp.int32),
            pltpu.VMEM((stored, width), jnp.bfloat16),
            pltpu.VMEM((rank, col_rows), jnp.bfloat16),
            pltpu.VMEM((n, halves, hc, width), jnp.bfloat16),
            pltpu.VMEM((n, hc, LANES), jnp.bfloat16),
            pltpu.VMEM((rank, KBLOCK), jnp.float32),
            pltpu.VMEM((I_DEV, KBLOCK), jnp.bfloat16),
            pltpu.SemaphoreType.DMA((2, n)),
            pltpu.SemaphoreType.DMA((2, n)),
            pltpu.SemaphoreType.DMA((2,)),
            pltpu.SemaphoreType.DMA((4,)),
        ],
        compiler_params=pltpu.CompilerParams(
            collective_id=0, has_side_effects=True, vmem_limit_bytes=32 * 1024 * 1024
        ),
        name="exchange",
    )(
        fiber_count,
        *(
            pltpu.with_memory_space_constraint(x, pltpu.HBM)
            for x in (
                fiber_i.reshape(1, stored),
                fiber_j.reshape(1, stored),
                fiber_rows,
                factor_two.T,
            )
        ),
    )
    per = 4
    return pl.pallas_call(
        functools.partial(contract_kernel, halves),
        out_shape=jax.ShapeDtypeStruct((I_DEV, rank * width), jnp.bfloat16),
        in_specs=[in_vmem, in_vmem, in_vmem],
        out_specs=pl.BlockSpec(memory_space=pl.ANY),
        scratch_shapes=[
            pltpu.VMEM((2, I_DEV, per * width), jnp.bfloat16),
            pltpu.VMEM((rank, KBLOCK), jnp.float32),
            pltpu.VMEM((I_DEV, KBLOCK), jnp.bfloat16),
            pltpu.SemaphoreType.DMA((2,)),
        ],
        compiler_params=pltpu.CompilerParams(vmem_limit_bytes=24 * 1024 * 1024),
        name="contract",
    )(got_rows, got_meta, total)


def solution(mesh):
    in_specs = (
        P(("row", "col"), None),
        P(("row", "col")),
        P(("row", "col")),
        P(("row", "col")),
        P("col", None),
    )
    out_specs = P(("row", "col"), None)
    step = functools.partial(body, mesh.shape["row"], mesh.shape["col"])
    return jax.shard_map(step, mesh=mesh, in_specs=in_specs, out_specs=out_specs, check_vma=False)
```

```python
import functools

import jax
import jax.numpy as jnp
from jax import lax
from jax.experimental import pallas as pl
from jax.experimental.pallas import tpu as pltpu
from jax.sharding import PartitionSpec as P

I_DEV = 128
LANES = 128
KBLOCK = 256
MESH = pl.DeviceIdType.MESH
ORDER = (1, 2, 3, 0)
ARRIVAL = (0, 1, 2, 3)


def contract_lanes(a, b):
    return lax.dot_general(a, b, (((1,), (1,)), ((), ())), preferred_element_type=jnp.float32)


def pack(
    n, cap, halves, count_ref, i_ref, j_ref, rows_ref, factor_ref, out_ref, meta_ref, ready
):
    stored = rows_ref.shape[0]
    rank, col_rows = factor_ref.shape
    ready[0].wait()
    index = i_ref[...]
    shift = I_DEV.bit_length() - 1
    target = jnp.right_shift(index, shift)
    local_i = jnp.bitwise_and(index, I_DEV - 1)
    live = lax.broadcasted_iota(jnp.int32, (1, stored), 1) < count_ref[0]
    target = jnp.where(live, target, -1)
    member = lax.broadcasted_iota(jnp.int32, (n, stored), 0) == target
    earlier = lax.broadcasted_iota(jnp.int32, (stored, stored), 0) < lax.broadcasted_iota(
        jnp.int32, (stored, stored), 1
    )
    before = jnp.dot(
        member.astype(jnp.float32).astype(jnp.bfloat16),
        earlier.astype(jnp.float32).astype(jnp.bfloat16),
        preferred_element_type=jnp.float32,
    )
    position = jnp.sum(jnp.where(member, before, 0.0), axis=0, keepdims=True).astype(jnp.int32)
    slot = jnp.where(live, target * cap + position, -1)

    ready[3].wait()
    fiber_rows = rows_ref[...]
    targets = KBLOCK // cap
    for step in range(n // targets):
        ids = lax.broadcasted_iota(jnp.int32, (KBLOCK, stored), 0) + step * KBLOCK
        move = (ids == slot).astype(jnp.float32).astype(jnp.bfloat16)
        moved = jnp.dot(move, fiber_rows, preferred_element_type=jnp.float32).astype(jnp.bfloat16)
        out_ref[step * targets : (step + 1) * targets] = moved.reshape(
            (targets,) + out_ref.shape[1:]
        )
    yield

    ready[1].wait()
    ready[2].wait()
    local_j = j_ref[...] - lax.axis_index("col") * col_rows
    high = jnp.right_shift(local_j, KBLOCK.bit_length() - 1)
    low = jnp.bitwise_and(local_j, KBLOCK - 1)
    chosen = lax.broadcasted_iota(jnp.int32, (KBLOCK, stored), 0) == low
    chosen = chosen.astype(jnp.float32).astype(jnp.bfloat16)
    pieces = col_rows // KBLOCK
    stacked = jnp.concatenate(
        [factor_ref[:, k * KBLOCK : (k + 1) * KBLOCK] for k in range(pieces)], axis=0
    )
    looked = jnp.dot(stacked, chosen, preferred_element_type=jnp.float32)
    own = jnp.zeros((rank, stored), jnp.float32)
    for k in range(pieces):
        own = own + jnp.where(high == k, looked[k * rank : (k + 1) * rank], 0.0)

    hc = cap // halves
    part = LANES // halves
    half = jnp.zeros_like(position)
    for h in range(1, halves):
        half = half + (position >= h * hc).astype(jnp.int32)
    half_slot = jnp.where(live, target * hc + position - half * hc, -1)
    place = jnp.broadcast_to(local_i.astype(jnp.float32), (8, stored))
    filler = jnp.zeros((part - rank - 8, stored), jnp.float32)
    chunks = []
    for h in range(halves):
        chunk = jnp.concatenate([own, place, filler], axis=0)
        chunks.append(jnp.where(half == h, chunk, 0.0))
    table = jnp.concatenate(chunks, axis=0).astype(jnp.bfloat16)
    spread = lax.broadcasted_iota(jnp.int32, (n * hc, stored), 0) == half_slot
    spread = spread.astype(jnp.float32).astype(jnp.bfloat16)
    meta_ref[...] = contract_lanes(spread, table).astype(jnp.bfloat16).reshape(meta_ref.shape)


def flip(z, g, groups):
    out = 0
    bit = 1
    while bit < groups:
        out = out + bit * ((z // bit + g // bit) % 2)
        bit *= 2
    return out


def expand(meta, halves, factor_ref, select_ref):
    span = meta.shape[0]
    rank = factor_ref.shape[0]
    part = LANES // halves
    turned = meta.astype(jnp.float32).T
    for h in range(halves):
        first = h * span
        factor_ref[:, first : first + span] = turned[h * part : h * part + rank]
        place = turned[h * part + rank : h * part + rank + 1]
        owned = lax.broadcasted_iota(jnp.int32, (I_DEV, span), 0).astype(jnp.float32)
        select_ref[:, first : first + span] = (
            (owned == place).astype(jnp.float32).astype(jnp.bfloat16)
        )


def spread_factors(select, factor_ref, first, count):
    return jnp.concatenate(
        [
            select * factor_ref[pl.ds(first + b, 1), :].astype(jnp.bfloat16)
            for b in range(count)
        ],
        axis=0,
    )


def exchange_kernel(
    nrow,
    ncol,
    groups,
    halves,
    count_ref,
    i_hbm,
    j_hbm,
    fiber_hbm,
    factor_hbm,
    rrows_ref,
    rmeta_ref,
    total_ref,
    i_ref,
    j_ref,
    fiber_ref,
    own_factor_ref,
    rows_ref,
    meta_ref,
    factor_ref,
    select_ref,
    send_sem,
    recv_sem,
    own_sem,
    in_sem,
):
    n = nrow * ncol
    members = n // groups
    per = ncol // groups
    r = lax.axis_index("row")
    c = lax.axis_index("col")
    me = r * ncol + c
    z, y = c // per, c % per
    seat = r * per + y

    barrier = pltpu.get_barrier_semaphore()

    def greet(k, _):
        other = (me + k) % n
        pl.semaphore_signal(
            barrier, inc=1, device_id=(other // ncol, other % ncol), device_id_type=MESH
        )
        return 0

    ready = (
        pltpu.make_async_copy(i_hbm, i_ref, in_sem.at[0]),
        pltpu.make_async_copy(j_hbm, j_ref, in_sem.at[1]),
        pltpu.make_async_copy(factor_hbm, own_factor_ref, in_sem.at[2]),
        pltpu.make_async_copy(fiber_hbm, fiber_ref, in_sem.at[3]),
    )
    for copy in ready:
        copy.start()
    lax.fori_loop(1, n, greet, 0)
    packing = pack(
        n,
        halves * rows_ref.shape[2],
        halves,
        count_ref,
        i_ref,
        j_ref,
        fiber_ref,
        own_factor_ref,
        rows_ref,
        meta_ref,
        ready,
    )
    next(packing)
    pl.semaphore_wait(barrier, n - 1)
    own_rows = pltpu.make_async_copy(rows_ref.at[me], rrows_ref.at[0, :, seat], own_sem.at[0])
    own_meta = pltpu.make_async_copy(meta_ref.at[me], rmeta_ref.at[0, seat], own_sem.at[1])

    def copies(g, k):
        tr = (r + k // per) % nrow
        tc = flip(z, g, groups) * per + (y + k % per) % per
        other = tr * ncol + tc
        t = g * members + k
        return (
            pltpu.make_async_remote_copy(
                src_ref=rows_ref.at[other],
                dst_ref=rrows_ref.at[g, :, seat],
                send_sem=send_sem.at[0, t],
                recv_sem=recv_sem.at[0, t],
                device_id=(tr, tc),
                device_id_type=MESH,
            ),
            pltpu.make_async_remote_copy(
                src_ref=meta_ref.at[other],
                dst_ref=rmeta_ref.at[g, seat],
                send_sem=send_sem.at[1, t],
                recv_sem=recv_sem.at[1, t],
                device_id=(tr, tc),
                device_id_type=MESH,
            ),
        )

    def send_all(g, which):
        def send(k, _):
            copies(g, k)[which].start()
            return 0

        lax.fori_loop(1 if g == 0 else 0, members, send, 0)

    send_all(ORDER[0], 0)
    next(packing, None)
    for g in ORDER:
        send_all(g, 1)
    for g in ORDER[1:]:
        send_all(g, 0)
    own_rows.start()
    own_meta.start()
    rank = factor_ref.shape[0]
    width = total_ref.shape[1]
    span = rmeta_ref.shape[1] * rmeta_ref.shape[2]
    kgroup = span * halves
    per_step = 8

    for place_in_order, g in enumerate(ARRIVAL):
        def arrive(k, _, g=g):
            for copy in copies(g, k):
                copy.wait_recv()
            return 0

        lax.fori_loop(1 if g == 0 else 0, members, arrive, 0)
        if g == 0:
            own_rows.wait()
            own_meta.wait()
        if place_in_order == groups - 1:
            break
        expand(rmeta_ref[g].reshape(span, LANES), halves, factor_ref, select_ref)

        def multiply(s, _, g=g, place_in_order=place_in_order):
            select = select_ref[...]
            left = spread_factors(select, factor_ref, s * per_step, per_step)
            product = jnp.dot(
                left, rrows_ref[g].reshape(kgroup, width), preferred_element_type=jnp.float32
            )
            span_m = per_step * I_DEV
            rows = pl.ds(pl.multiple_of(s * span_m, span_m), span_m)
            if place_in_order > 0:
                product = product + total_ref[rows, :]
            total_ref[rows, :] = product
            return 0

        lax.fori_loop(0, rank // per_step, multiply, 0)

    for g in ORDER:
        def finish(k, _, g=g):
            for copy in copies(g, k):
                copy.wait_send()
            return 0

        lax.fori_loop(1 if g == 0 else 0, members, finish, 0)


def contract_kernel(
    halves, rows_ref, meta_ref, total_ref, out_ref, stage_ref, factor_ref, select_ref, sem
):
    last = ARRIVAL[-1]
    rank, kgroup = factor_ref.shape
    width = total_ref.shape[1]
    per = stage_ref.shape[2] // width
    steps = rank // per
    expand(meta_ref[last].reshape(kgroup // halves, LANES), halves, factor_ref, select_ref)

    def copy_out(s, slot):
        at = pl.multiple_of(s * per * width, per * width)
        return pltpu.make_async_copy(
            stage_ref.at[slot], out_ref.at[:, pl.ds(at, per * width)], sem.at[slot]
        )

    def multiply(s, _):
        slot = s % 2

        @pl.when(s >= 2)
        def _():
            copy_out(s - 2, slot).wait()

        left = spread_factors(select_ref[...], factor_ref, s * per, per)
        product = jnp.dot(
            left, rows_ref[last].reshape(kgroup, width), preferred_element_type=jnp.float32
        )
        span_m = per * I_DEV
        product = product + total_ref[pl.ds(pl.multiple_of(s * span_m, span_m), span_m), :]
        for b in range(per):
            stage_ref[slot, :, b * width : (b + 1) * width] = product[
                b * I_DEV : (b + 1) * I_DEV
            ].astype(jnp.bfloat16)
        copy_out(s, slot).start()
        return 0

    lax.fori_loop(0, steps, multiply, 0)
    copy_out(steps - 2, steps % 2).wait()
    copy_out(steps - 1, (steps - 1) % 2).wait()


def body(nrow, ncol, fiber_rows, fiber_i, fiber_j, fiber_count, factor_two):
    n = nrow * ncol
    stored, width = fiber_rows.shape
    col_rows, rank = factor_two.shape
    cap = 2 * stored // n
    slots = n * cap
    halves = 2 if cap % 32 == 0 else 1
    hc = cap // halves
    groups = slots // KBLOCK
    members = n // groups
    in_vmem = pl.BlockSpec(memory_space=pltpu.VMEM)
    got_rows, got_meta, total = pl.pallas_call(
        functools.partial(exchange_kernel, nrow, ncol, groups, halves),
        out_shape=(
            jax.ShapeDtypeStruct((groups, halves, members, hc, width), jnp.bfloat16),
            jax.ShapeDtypeStruct((groups, members, hc, LANES), jnp.bfloat16),
            jax.ShapeDtypeStruct((I_DEV * rank, width), jnp.float32),
        ),
        in_specs=[pl.BlockSpec(memory_space=pltpu.SMEM)] + [pl.BlockSpec(memory_space=pltpu.HBM)] * 4,
        out_specs=(in_vmem, in_vmem, in_vmem),
        scratch_shapes=[
            pltpu.VMEM((1, stored), jnp.int32),
            pltpu.VMEM((1, stored), jnp.int32),
            pltpu.VMEM((stored, width), jnp.bfloat16),
            pltpu.VMEM((rank, col_rows), jnp.bfloat16),
            pltpu.VMEM((n, halves, hc, width), jnp.bfloat16),
            pltpu.VMEM((n, hc, LANES), jnp.bfloat16),
            pltpu.VMEM((rank, KBLOCK), jnp.float32),
            pltpu.VMEM((I_DEV, KBLOCK), jnp.bfloat16),
            pltpu.SemaphoreType.DMA((2, n)),
            pltpu.SemaphoreType.DMA((2, n)),
            pltpu.SemaphoreType.DMA((2,)),
            pltpu.SemaphoreType.DMA((4,)),
        ],
        compiler_params=pltpu.CompilerParams(
            collective_id=0, has_side_effects=True, vmem_limit_bytes=32 * 1024 * 1024
        ),
        name="exchange",
    )(
        fiber_count,
        *(
            pltpu.with_memory_space_constraint(x, pltpu.HBM)
            for x in (
                fiber_i.reshape(1, stored),
                fiber_j.reshape(1, stored),
                fiber_rows,
                factor_two.T,
            )
        ),
    )
    per = 4
    return pl.pallas_call(
        functools.partial(contract_kernel, halves),
        out_shape=jax.ShapeDtypeStruct((I_DEV, rank * width), jnp.bfloat16),
        in_specs=[in_vmem, in_vmem, in_vmem],
        out_specs=pl.BlockSpec(memory_space=pl.ANY),
        scratch_shapes=[
            pltpu.VMEM((2, I_DEV, per * width), jnp.bfloat16),
            pltpu.VMEM((rank, KBLOCK), jnp.float32),
            pltpu.VMEM((I_DEV, KBLOCK), jnp.bfloat16),
            pltpu.SemaphoreType.DMA((2,)),
        ],
        compiler_params=pltpu.CompilerParams(vmem_limit_bytes=24 * 1024 * 1024),
        name="contract",
    )(got_rows, got_meta, total)


def solution(mesh):
    in_specs = (
        P(("row", "col"), None),
        P(("row", "col")),
        P(("row", "col")),
        P(("row", "col")),
        P("col", None),
    )
    out_specs = P(("row", "col"), None)
    step = functools.partial(body, mesh.shape["row"], mesh.shape["col"])
    return jax.shard_map(step, mesh=mesh, in_specs=in_specs, out_specs=out_specs, check_vma=False)
```
